1024 devices in a mesh: wide: 16 (over z_lo, core), narrow: 64 (over z_hi, x, y).
Axes of the slice: x: 4, y: 8, z: 16 (z_hi: 2, z_lo: 8; z = z_hi * 8 + z_lo), core: 2. Of those that a mesh axis runs over, the one named last changes fastest.
Arguments:
- amplitudes: float32 [16, 64, 16, 1, 64, 128], P('wide', 'narrow'), may hold values from -6 to 6
- gate_bank: float32 [16, 128, 128], replicated, may hold values from -1 to 1, as said below
- gate_pick: int32 [34], replicated, may hold values from 0 to 15
Outputs:
- evolved: float32 [16, 64, 16, 1, 64, 128], P('wide', 'narrow')
The draws below stay inside these ranges and needn't reach their ends.
Inputs may be any that keep to these rules, and one draw needn't show every extreme that they name: `gate_bank`: every matrix of the bank is orthogonal.
All inputs are finite; a program needn't handle non-finite values.
Results may differ from the reference program's by a relative error of at most 0.00014.
Values sent between devices are 32-bit elements; how exact they have to be, the bound alone decides.
A program may use at most 32 MiB of HBM per device.

```python
import jax
import jax.numpy as jnp
from jax import lax

GATE = 128
SPARE = 1
BANK = 16
PICKS = 34
N_WIDE = 16
N_NARROW = 64


def draw_gate_bank(key, part):
    raw = jax.random.normal(key, (BANK, GATE, GATE), jnp.float32)
    factor, upper = jnp.linalg.qr(raw)
    return factor


def with_ends(values, stream_key, least, high):
    place = [jax.random.randint(jax.random.fold_in(stream_key, axis), (), 0, length) for axis, length in enumerate(values.shape)]
    longest = values.shape.index(max(values.shape))
    beside = place[:longest] + [(place[longest] + 1) % values.shape[longest]] + place[longest + 1:]
    return values.at[tuple(place)].set(least).at[tuple(beside)].set(high)


def block_scale(key, shape, cuts, smallest, top_value):
    loudness = 1.0
    for position, blocks in cuts:
        heights = jax.random.uniform(jax.random.fold_in(jax.random.fold_in(key, 6), position), (blocks,), jnp.float32, smallest / len(cuts), top_value / len(cuts))
        loudness = loudness * jnp.repeat(jnp.exp(heights), shape[position] // blocks).reshape((-1,) + (1,) * (len(shape) - 1 - position))
    return loudness


def noise(stream_key, shape, spread, most, cuts=(), dtype=jnp.bfloat16):
    values = jax.random.normal(stream_key, shape, jnp.float32) * spread
    if len(cuts) > 0:
        values = block_scale(stream_key, shape, cuts, -0.22, 0.18) * values
    return jnp.clip(values, min=-most, max=most).astype(dtype)


def setup_inputs(seed: int = 0) -> dict:
    keys = jax.random.split(jax.random.key(seed), 4)
    amplitudes = noise(keys[0], (N_WIDE, N_NARROW, N_WIDE, SPARE, GATE // 2, GATE), 1.0, 6.0, ((0, 16), (1, 64)), jnp.float32)
    gate_bank = draw_gate_bank(jax.random.fold_in(keys[3], 71), 0)
    gate_pick = with_ends(jax.random.randint(keys[2], (PICKS,), 0, BANK), jax.random.fold_in(keys[2], 1), 0, BANK - 1).astype(jnp.int32)
    return {"amplitudes": amplitudes, "gate_bank": gate_bank, "gate_pick": gate_pick}


def reference(amplitudes, gate_bank, gate_pick):
    levels = N_NARROW.bit_length() - 1
    half_width = GATE // 2
    local_width = GATE // N_WIDE
    highest = lax.Precision.HIGHEST

    def apply_local(vector, layer_index):
        matrices = jnp.take(gate_bank, gate_pick[4 * layer_index:4 * layer_index + 4], axis=0)
        split = vector.reshape(N_WIDE, N_NARROW, 4, N_WIDE // 4, SPARE, half_width, GATE)
        result = jnp.einsum('wnhcsba,hae->wnhcsbe', split, matrices, precision=highest)
        return result.reshape(vector.shape)

    def apply_narrow(vector, bit_index, pick_index):
        blocks = gate_bank[gate_pick[pick_index]].reshape(2, half_width, 2, half_width)
        split = vector.reshape(N_WIDE, N_NARROW // 2 ** (bit_index + 1), 2, 2 ** bit_index, N_WIDE, SPARE, half_width, GATE)
        result = jnp.einsum('wpgqcsba,gbhd->wphqcsda', split, blocks, precision=highest)
        return result.reshape(vector.shape)

    def apply_wide(vector, pick_index):
        blocks = gate_bank[gate_pick[pick_index]].reshape(N_WIDE, local_width, N_WIDE, local_width)
        split = vector.reshape(N_WIDE, N_NARROW, N_WIDE, SPARE, half_width // local_width, local_width, GATE)
        result = jnp.einsum('wncsbqa,wqvr->vncsbra', split, blocks, precision=highest)
        return result.reshape(vector.shape)
    vector = amplitudes
    vector = apply_local(vector, 0)
    vector = apply_wide(vector, 32)
    vector = apply_local(vector, 1)
    vector = apply_narrow(vector, 0, 28)
    vector = apply_local(vector, 2)
    vector = apply_narrow(vector, levels - 1, 29)
    vector = apply_local(vector, 3)
    vector = apply_wide(vector, 33)
    vector = apply_local(vector, 4)
    vector = apply_narrow(vector, 1, 30)
    vector = apply_local(vector, 5)
    vector = apply_narrow(vector, levels - 2, 31)
    vector = apply_local(vector, 6)
    return vector
```

```python
import jax
import jax.numpy as jnp
from jax import lax
from jax.sharding import PartitionSpec as P

GATE = 128
HIGHEST = lax.Precision.HIGHEST


def groups_of(wide_count, narrow_count, active):
    levels = narrow_count.bit_length() - 1
    idle = [bit for bit in range(levels) if bit not in active]
    groups = []
    for spectator in range(2 ** len(idle)):
        base = sum((spectator >> i & 1) << bit for i, bit in enumerate(idle))
        group = []
        for w in range(wide_count):
            for sub in range(2 ** len(active)):
                n = base + sum((sub >> i & 1) << bit for i, bit in enumerate(active))
                group.append(w * narrow_count + n)
        groups.append(group)
    return groups


def per_device(amplitudes, gate_bank, gate_pick):
    gates = gate_bank[gate_pick]
    local = gates[:28].reshape(7, 4, GATE, GATE)
    merged = local[0]
    for layer in range(1, 7):
        merged = jnp.einsum("hab,hbc->hac", merged, local[layer], precision=HIGHEST)
    groups = groups_of(16, 64, (0, 1, 4, 5))
    x = jnp.einsum("hra,hae->hre", amplitudes.reshape(4, -1, GATE), merged, precision=HIGHEST)
    x = x.reshape(16, 64, 16, 8).transpose(0, 2, 1, 3).reshape(256, 64, 8)
    x = lax.all_to_all(x, ("wide", "narrow"), 0, 0, axis_index_groups=groups, tiled=True)
    x = x.reshape(16, 2, 2, 2, 2, 8, 8, 8)
    wide1 = gates[32].reshape(16, 8, 16, 8)
    wide2 = gates[33].reshape(16, 8, 16, 8)
    n28, n29, n30, n31 = (gates[i].reshape(2, 8, 8, 2, 8, 8) for i in (28, 29, 30, 31))
    x = jnp.einsum("wijklbqa,wqvr->vijklbra", x, wide1, precision=HIGHEST)
    x = jnp.einsum("wijklbqa,lbqmcr->wijkmcra", x, n28, precision=HIGHEST)
    x = jnp.einsum("wijklbqa,ibqmcr->wmjklcra", x, n29, precision=HIGHEST)
    x = jnp.einsum("wijklbqa,wqvr->vijklbra", x, wide2, precision=HIGHEST)
    x = jnp.einsum("wijklbqa,kbqmcr->wijmlcra", x, n30, precision=HIGHEST)
    x = jnp.einsum("wijklbqa,jbqmcr->wimklcra", x, n31, precision=HIGHEST)
    x = x.reshape(256, 64, 8)
    x = lax.all_to_all(x, ("wide", "narrow"), 0, 0, axis_index_groups=groups, tiled=True)
    x = x.reshape(16, 16, 64, 8).transpose(0, 2, 1, 3)
    return x.reshape(amplitudes.shape)


def solution(mesh):
    placed = (P("wide", "narrow", None, None, None, None), P(), P())
    return jax.shard_map(
        per_device,
        mesh=mesh,
        in_specs=placed,
        out_specs=P("wide", "narrow", None, None, None, None),
        check_vma=False,
    )
```

```python
import functools

import jax
import jax.numpy as jnp
from jax import lax
from jax.experimental import pallas as pl
from jax.experimental.pallas import tpu as pltpu
from jax.sharding import PartitionSpec as P

GATE = 128
CHUNKS = 4
FAR = 32
NEAR = 8
MESH = pl.DeviceIdType.MESH
ROWS_IN = ["r1", "r0", "b2", "b1", "b0"]
LANES_IN = ["a6", "a5", "a4", "a3", "a2", "a1", "a0"]


def swap(x, row_bit, lane_bit):
    outer, inner, apart = 16 >> row_bit, 8 << row_bit, 1 << lane_bit
    split = x.reshape(outer, 2, inner, 128)
    low, high = split[:, 0].reshape(128, 128), split[:, 1].reshape(128, 128)
    clear = lax.broadcasted_iota(jnp.int32, (128, 128), 1) // apart % 2 == 0
    new_low = jnp.where(clear, low, pltpu.roll(high, apart, 1))
    new_high = jnp.where(clear, pltpu.roll(low, 128 - apart, 1), high)
    parts = [new_low.reshape(outer, 1, inner, 128), new_high.reshape(outer, 1, inner, 128)]
    return jnp.concatenate(parts, axis=1).reshape(32, 8, 128)


class Layout:
    def __init__(self, rows, lanes):
        self.rows, self.lanes = list(rows), list(lanes)

    def exchange(self, x, pairs):
        for row, lane in pairs:
            i, p = self.rows.index(row), self.lanes.index(lane)
            x = swap(x, 4 - i, 6 - p)
            self.rows[i], self.lanes[p] = lane, row
        return x


def halves(x):
    top = x.astype(jnp.bfloat16)
    return top, (x - top.astype(jnp.float32)).astype(jnp.bfloat16)


def product(left, right):
    dot = functools.partial(jnp.dot, preferred_element_type=jnp.float32)
    return dot(left[0], right[0]) + (dot(left[0], right[1]) + dot(left[1], right[0]))


def gate_low(x, matrix):
    wide = jnp.concatenate([x[:16].reshape(128, 128), x[16:].reshape(128, 128)], axis=1)
    y = product(matrix, halves(wide))
    return jnp.concatenate([y[:, :128].reshape(16, 8, 128), y[:, 128:].reshape(16, 8, 128)], axis=0)


def gate_high(x, matrix):
    split = x.reshape(4, 64, 128)
    first = jnp.concatenate([split[0], split[2]], axis=0)
    second = jnp.concatenate([split[1], split[3]], axis=0)
    y = product(matrix, halves(jnp.concatenate([first, second], axis=1)))
    parts = [y[:64, :128], y[:64, 128:], y[64:, :128], y[64:, 128:]]
    return jnp.concatenate([part.reshape(8, 8, 128) for part in parts], axis=0)


def stage_a(x):
    at = Layout(ROWS_IN, LANES_IN)
    x = at.exchange(x, [("b2", "a6"), ("b1", "a5"), ("b0", "a4")])
    return x


def stage_b(x, matrix):
    at = Layout(["zh", "z2", "z1", "z0", "co"], ["b2", "b1", "b0", "a3", "a2", "a1", "a0"])
    x = gate_low(x, matrix(0))
    return at.exchange(x, [("zh", "a3"), ("z2", "a2"), ("z1", "a1")])


def stage_c(x, matrix):
    at = Layout(["x1", "y0", "y1", "z0", "co"], ["b2", "b1", "b0", "zh", "z2", "z1", "a0"])
    x = at.exchange(x, [("x1", "zh"), ("y1", "b2"), ("z0", "b1"), ("co", "b0")])
    assert at.rows == ["zh", "y0", "b2", "b1", "b0"]
    x = gate_low(x, matrix(1))
    x = gate_high(x, matrix(2))
    x = at.exchange(x, [("y0", "z2"), ("b2", "z1"), ("b1", "z0"), ("b0", "co")])
    assert at.rows == ["zh", "z2", "z1", "z0", "co"]
    x = gate_low(x, matrix(3))
    x = at.exchange(x, [("zh", "x1"), ("z2", "y1"), ("z1", "b2"), ("z0", "b1"), ("co", "b0")])
    assert at.rows == ["x1", "y1", "b2", "b1", "b0"]
    x = gate_low(x, matrix(4))
    x = gate_high(x, matrix(5))
    x = at.exchange(x, [("b2", "y0")])
    assert at.lanes == ["z2", "z0", "co", "zh", "b2", "z1", "a0"]
    return x


def stage_d(x):
    at = Layout(["a3", "a1", "a2", "b1", "b0"], ["z2", "z0", "co", "zh", "b2", "z1", "a0"])
    x = at.exchange(x, [("a3", "zh"), ("a1", "z2"), ("a2", "z1"), ("b1", "z0"), ("b0", "co")])
    assert at.rows == ["zh", "z2", "z1", "z0", "co"]
    assert at.lanes == ["a1", "b1", "b0", "a3", "b2", "a2", "a0"]
    return x


def stage_e(x, merged):
    at = Layout(["r1", "r0", "a6", "a5", "a4"], ["a1", "b1", "b0", "a3", "b2", "a2", "a0"])
    x = at.exchange(x, [("a6", "b2"), ("a5", "b1"), ("a4", "b0")])
    assert at.rows == ROWS_IN
    assert at.lanes == ["a1", "a5", "a4", "a3", "a6", "a2", "a0"]
    return product(halves(x.reshape(256, 128)), merged)


def lane_order():
    lane = lax.broadcasted_iota(jnp.int32, (128, 128), 0)
    a = 0
    for place, bit in zip((6, 5, 4, 3, 2, 1, 0), (1, 5, 4, 3, 6, 2, 0)):
        a = a + lane // 2**place % 2 * 2**bit
    return jnp.where(lax.broadcasted_iota(jnp.int32, (128, 128), 1) == a, 1.0, 0.0)


def kernel(
    pick_ref, x_ref, bank_ref, o_ref,
    far_out, far_in, near_out, near_in, near_back, near_got, far_back, far_got,
    turned, merged, send_sem, recv_sem,
):
    w, n = lax.axis_index("wide"), lax.axis_index("narrow")
    me_far = n // 32 * 16 + w
    me_near = n // 16 % 2 * 4 + n % 2 * 2 + n // 2 % 2
    me_back = n // 16 % 2 * 4 + n // 2 % 2 * 2 + n % 2
    rest = n - n // 16 % 2 * 16 - n % 4

    def far_device(d):
        return {"wide": d % 16, "narrow": d // 16 * 32 + n % 32}

    def near_device(e):
        return {"wide": w, "narrow": rest + e // 4 * 16 + e % 2 * 2 + e // 2 % 2}

    def back_device(e):
        return {"wide": w, "narrow": rest + e // 4 * 16 + e % 4}

    barrier = pltpu.get_barrier_semaphore()

    def greet_far(k, carry):
        pl.semaphore_signal(barrier, inc=1, device_id=far_device((me_far + k) % FAR), device_id_type=MESH)
        return carry

    def greet_near(k, carry):
        pl.semaphore_signal(barrier, inc=1, device_id=near_device((me_near + k) % NEAR), device_id_type=MESH)
        return carry

    lax.fori_loop(1, FAR, greet_far, 0)
    lax.fori_loop(1, NEAR, greet_near, 0)

    def send(count, me, device, source, target, kind, chunk):
        def one(j, carry):
            k = count // 2 + j // 2 * (1 - j % 2) - (j + 1) // 2 * (j % 2)
            d = (me + k) % count
            pltpu.make_async_remote_copy(
                src_ref=source.at[chunk, d],
                dst_ref=target.at[chunk, me],
                send_sem=send_sem.at[kind, chunk],
                recv_sem=recv_sem.at[kind, chunk],
                device_id=device(d),
                device_id_type=MESH,
            ).start()
            return carry

        lax.fori_loop(0, count - 1, one, 0)
        target[chunk, me] = source[chunk, me]

    def whole(count, me, device, source, target, kind, chunk):
        return pltpu.make_async_remote_copy(
            src_ref=source.at[chunk, pl.ds(0, count - 1)],
            dst_ref=target.at[chunk, pl.ds(0, count - 1)],
            send_sem=send_sem.at[kind, chunk],
            recv_sem=recv_sem.at[kind, chunk],
            device_id=device((me + 1) % count),
            device_id_type=MESH,
        )

    trades = [
        (FAR, me_far, far_device, far_out, far_in, 0),
        (NEAR, me_near, near_device, near_out, near_in, 1),
        (NEAR, me_back, back_device, near_back, near_got, 2),
        (FAR, me_far, far_device, far_back, far_got, 3),
    ]

    def matrix(index):
        return turned[0, index], turned[1, index]

    for chunk in range(CHUNKS):
        far_out[chunk] = stage_a(x_ref[chunk])
    for index in range(6):
        pick = (32, 28, 29, 33, 30, 31)[index]
        top, rest_of = halves(bank_ref[pick_ref[pick]].T)
        turned[0, index], turned[1, index] = top, rest_of

    pl.semaphore_wait(barrier, FAR + NEAR - 2)
    for chunk in range(CHUNKS):
        send(*trades[0], chunk)

    order = halves(lane_order())

    def merge(h, carry):
        layers = [halves(bank_ref[pick_ref[4 * layer + h]]) for layer in range(7)]
        total = product(order, layers[0])
        for layer in range(1, 7):
            total = product(halves(total), layers[layer])
        merged[0, h], merged[1, h] = halves(total)
        return carry

    lax.fori_loop(0, CHUNKS, merge, 0)

    def run_b(chunk):
        whole(*trades[0], chunk).wait_recv()
        near_out[chunk] = stage_b(far_in[chunk], matrix).reshape(8, 4, 8, 128)
        send(*trades[1], chunk)

    def run_c(chunk):
        whole(*trades[1], chunk).wait_recv()
        near_back[chunk] = stage_c(near_in[chunk].reshape(32, 8, 128), matrix).reshape(8, 4, 8, 128)
        send(*trades[2], chunk)

    def run_d(chunk):
        whole(*trades[2], chunk).wait_recv()
        far_back[chunk] = stage_d(near_got[chunk].reshape(32, 8, 128))
        send(*trades[3], chunk)

    def run_e(chunk):
        whole(*trades[3], chunk).wait_recv()
        o_ref[chunk] = stage_e(far_got[chunk], (merged[0, chunk], merged[1, chunk])).reshape(32, 8, 128)

    stages = {"b": run_b, "c": run_c, "d": run_d, "e": run_e}
    for step in "b0 b1 c0 b2 c1 d0 b3 c2 d1 c3 d2 e0 d3 e1 e2 e3".split():
        stages[step[0]](int(step[1]))
    for trade in trades:
        for chunk in range(CHUNKS):
            whole(*trade, chunk).wait_send()


def per_device(amplitudes, gate_bank, gate_pick):
    far = pltpu.VMEM((CHUNKS, FAR, 8, 128), jnp.float32)
    near = pltpu.VMEM((CHUNKS, NEAR, 4, 8, 128), jnp.float32)
    result = pl.pallas_call(
        kernel,
        out_shape=jax.ShapeDtypeStruct((CHUNKS, 32, 8, 128), jnp.float32),
        in_specs=[
            pl.BlockSpec(memory_space=pltpu.SMEM),
            pl.BlockSpec(memory_space=pltpu.VMEM),
            pl.BlockSpec(memory_space=pltpu.VMEM),
        ],
        out_specs=pl.BlockSpec(memory_space=pltpu.VMEM),
        scratch_shapes=[
            far, far, near, near, near, near, far, far,
            pltpu.VMEM((2, 6, GATE, GATE), jnp.bfloat16),
            pltpu.VMEM((2, CHUNKS, GATE, GATE), jnp.bfloat16),
            pltpu.SemaphoreType.DMA((4, CHUNKS)),
            pltpu.SemaphoreType.DMA((4, CHUNKS)),
        ],
        compiler_params=pltpu.CompilerParams(
            collective_id=0, has_side_effects=True, vmem_limit_bytes=32 << 20
        ),
    )(gate_pick, amplitudes.reshape(CHUNKS, 32, 8, 128), gate_bank)
    return result.reshape(amplitudes.shape)


def solution(mesh):
    placed = (P("wide", "narrow", None, None, None, None), P(), P())
    return jax.shard_map(
        per_device,
        mesh=mesh,
        in_specs=placed,
        out_specs=P("wide", "narrow", None, None, None, None),
        check_vma=False,
    )
```

```python
import functools

import jax
import jax.numpy as jnp
from jax import lax
from jax.experimental import pallas as pl
from jax.experimental.pallas import tpu as pltpu
from jax.sharding import PartitionSpec as P

GATE = 128
CHUNKS = 4
FAR = 32
NEAR = 8
FAR_FIRST = (0, 1)
MESH = pl.DeviceIdType.MESH
ROWS_IN = ["r1", "r0", "b2", "b1", "b0"]
LANES_IN = ["a6", "a5", "a4", "a3", "a2", "a1", "a0"]
LANES_OUT = ["a1", "a5", "a4", "a3", "a6", "a2", "a0"]
FAR_ROWS = ["zh", "z2", "z1", "z0", "co"]


def swap(x, row_bit, lane_bit):
    outer, inner, apart = 16 >> row_bit, 8 << row_bit, 1 << lane_bit
    split = x.reshape(outer, 2, inner, 128)
    low, high = split[:, 0].reshape(128, 128), split[:, 1].reshape(128, 128)
    clear = lax.broadcasted_iota(jnp.int32, (128, 128), 1) // apart % 2 == 0
    new_low = jnp.where(clear, low, pltpu.roll(high, apart, 1))
    new_high = jnp.where(clear, pltpu.roll(low, 128 - apart, 1), high)
    parts = [new_low.reshape(outer, 1, inner, 128), new_high.reshape(outer, 1, inner, 128)]
    return jnp.concatenate(parts, axis=1).reshape(32, 8, 128)


class Layout:
    def __init__(self, rows, lanes):
        self.rows, self.lanes = list(rows), list(lanes)

    def exchange(self, x, pairs):
        for row, lane in pairs:
            i, p = self.rows.index(row), self.lanes.index(lane)
            x = swap(x, 4 - i, 6 - p)
            self.rows[i], self.lanes[p] = lane, row
        return x


def halves(x):
    top = x.astype(jnp.bfloat16)
    return top, (x - top.astype(jnp.float32)).astype(jnp.bfloat16)


def product(left, right):
    dot = functools.partial(jnp.dot, preferred_element_type=jnp.float32)
    return dot(left[0], right[0]) + (dot(left[0], right[1]) + dot(left[1], right[0]))


def gate_low(x, matrix):
    wide = jnp.concatenate([x[:16].reshape(128, 128), x[16:].reshape(128, 128)], axis=1)
    y = product(matrix, halves(wide))
    return jnp.concatenate([y[:, :128].reshape(16, 8, 128), y[:, 128:].reshape(16, 8, 128)], axis=0)


def gate_high(x, matrix):
    split = x.reshape(4, 64, 128)
    first = jnp.concatenate([split[0], split[2]], axis=0)
    second = jnp.concatenate([split[1], split[3]], axis=0)
    y = product(matrix, halves(jnp.concatenate([first, second], axis=1)))
    parts = [y[:64, :128], y[:64, 128:], y[64:, :128], y[64:, 128:]]
    return jnp.concatenate([part.reshape(8, 8, 128) for part in parts], axis=0)


def first_far(x):
    at = Layout(ROWS_IN, LANES_IN)
    return at.exchange(x, [("b2", "a6"), ("b1", "a5"), ("b0", "a4")])


def first_near(x):
    at = Layout(ROWS_IN, LANES_IN)
    x = at.exchange(x, [("r1", "a3"), ("r0", "a2"), ("b2", "a1")])
    assert at.rows == ["a3", "a2", "a1", "b1", "b0"]
    return x


def near_then_far(x):
    at = Layout(["x1", "y0", "y1", "b1", "b0"], ["a6", "a5", "a4", "r1", "r0", "b2", "a0"])
    x = at.exchange(x, [("x1", "r1"), ("y0", "r0"), ("y1", "a6"), ("b1", "a5"), ("b0", "a4")])
    assert at.rows == ["r1", "r0", "a6", "a5", "a4"]
    assert at.lanes == ["y1", "b1", "b0", "x1", "y0", "b2", "a0"]
    return x


def far_then_near(x, matrix):
    at = Layout(FAR_ROWS, ["b2", "b1", "b0", "a3", "a2", "a1", "a0"])
    x = gate_low(x, matrix(0))
    return at.exchange(x, [("zh", "a3"), ("z2", "a2"), ("z1", "a1")])


def gates_between(at, x, matrix):
    assert at.rows == ["zh", "y0", "b2", "b1", "b0"]
    assert at.lanes == ["y1", "z0", "co", "x1", "z2", "z1", "a0"]
    x = gate_low(x, matrix(1))
    x = gate_high(x, matrix(2))
    x = at.exchange(x, [("y0", "z2"), ("b2", "z1"), ("b1", "z0"), ("b0", "co")])
    assert at.rows == FAR_ROWS
    x = gate_low(x, matrix(3))
    x = at.exchange(x, [("zh", "x1"), ("z2", "y1"), ("z1", "b2"), ("z0", "b1"), ("co", "b0")])
    assert at.rows == ["x1", "y1", "b2", "b1", "b0"]
    x = gate_low(x, matrix(4))
    return gate_high(x, matrix(5))


def gates_from_near(x, matrix):
    at = Layout(["x1", "y0", "y1", "z0", "co"], ["b2", "b1", "b0", "zh", "z2", "z1", "a0"])
    x = at.exchange(x, [("x1", "zh"), ("y1", "b2"), ("z0", "b1"), ("co", "b0")])
    x = gates_between(at, x, matrix)
    x = at.exchange(x, [("x1", "zh"), ("y1", "z2"), ("b2", "z1"), ("b1", "z0"), ("b0", "co")])
    assert at.rows == FAR_ROWS
    assert at.lanes == ["y1", "b1", "b0", "x1", "y0", "b2", "a0"]
    return x


def gates_from_far(x, matrix):
    at = Layout(FAR_ROWS, ["y1", "b1", "b0", "x1", "y0", "b2", "a0"])
    x = gate_low(x, matrix(0))
    x = at.exchange(x, [("z2", "y0"), ("z1", "b2"), ("z0", "b1"), ("co", "b0")])
    x = gates_between(at, x, matrix)
    x = at.exchange(x, [("b2", "y0")])
    assert at.lanes == ["z2", "z0", "co", "zh", "b2", "z1", "a0"]
    return x


def back_near(x):
    at = Layout(["r1", "r0", "a6", "a5", "a4"], ["y1", "b1", "b0", "x1", "y0", "b2", "a0"])
    x = at.exchange(x, [("r1", "x1"), ("r0", "y1"), ("a6", "y0")])
    assert at.lanes == ["r0", "b1", "b0", "r1", "a6", "b2", "a0"]
    return x


def back_far(x):
    at = Layout(["a3", "a1", "a2", "b1", "b0"], ["z2", "z0", "co", "zh", "b2", "z1", "a0"])
    x = at.exchange(x, [("a3", "zh"), ("a1", "z2"), ("a2", "z1"), ("b1", "z0"), ("b0", "co")])
    assert at.rows == FAR_ROWS
    assert at.lanes == ["a1", "b1", "b0", "a3", "b2", "a2", "a0"]
    return x


def last_from_far(x, merged):
    at = Layout(["r1", "r0", "a6", "a5", "a4"], ["a1", "b1", "b0", "a3", "b2", "a2", "a0"])
    x = at.exchange(x, [("a6", "b2"), ("a5", "b1"), ("a4", "b0")])
    assert at.rows == ROWS_IN and at.lanes == LANES_OUT
    return product(halves(x.reshape(256, 128)), merged)


def last_from_near(x, merged):
    at = Layout(["a3", "a1", "a2", "a5", "a4"], ["r0", "b1", "b0", "r1", "a6", "b2", "a0"])
    x = at.exchange(x, [("a3", "r1"), ("a1", "r0"), ("a2", "b2"), ("a5", "b1"), ("a4", "b0")])
    assert at.rows == ROWS_IN and at.lanes == LANES_OUT
    return product(halves(x.reshape(256, 128)), merged)


def lane_order():
    lane = lax.broadcasted_iota(jnp.int32, (128, 128), 0)
    a = 0
    for place, bit in zip((6, 5, 4, 3, 2, 1, 0), (1, 5, 4, 3, 6, 2, 0)):
        a = a + lane // 2**place % 2 * 2**bit
    return jnp.where(lax.broadcasted_iota(jnp.int32, (128, 128), 1) == a, 1.0, 0.0)


def kernel(
    pick_hbm, x_hbm, bank_hbm, o_hbm,
    pick_ref, x_ref, bank_ref,
    far_out, far_in, near_out, near_in, near_back, near_got, far_back, far_got,
    turned, merged, load_sem, send_sem, recv_sem,
):
    w, n = lax.axis_index("wide"), lax.axis_index("narrow")
    me_far = n // 32 * 16 + w
    me_near = n // 16 % 2 * 4 + n % 2 * 2 + n // 2 % 2
    me_back = n // 16 % 2 * 4 + n // 2 % 2 * 2 + n % 2
    rest = n - n // 16 % 2 * 16 - n % 4

    column = n % 32

    def far_device(d):
        upper = jnp.where(d >= 16, 1, 0)
        return {"wide": d - upper * 16, "narrow": column + upper * 32}

    def near_bits(e):
        top = jnp.where(e >= 4, 1, 0)
        low = e - top * 4
        middle = jnp.where(low >= 2, 1, 0)
        return top, middle, low - middle * 2

    def near_device(e):
        top, middle, low = near_bits(e)
        return {"wide": w, "narrow": rest + top * 16 + low * 2 + middle}

    def back_device(e):
        top, middle, low = near_bits(e)
        return {"wide": w, "narrow": rest + top * 16 + middle * 2 + low}

    def around(count, me, each):
        def at(d):
            each(jnp.where(d >= count, d - count, d))

        at(me + count // 2)
        most = count // 2 - 1

        def some(i, carry):
            for step in range(3):
                near = 3 * i + step
                at(me + most - near)
                at(me + count - most + near)
            return carry

        lax.fori_loop(0, most // 3, some, 0)

    barrier = pltpu.get_barrier_semaphore()

    def greet(device):
        pl.semaphore_signal(barrier, inc=1, device_id=device, device_id_type=MESH)

    around(FAR, me_far, lambda d: greet(far_device(d)))
    around(NEAR, me_near, lambda d: greet(near_device(d)))

    loads = [
        pltpu.make_async_copy(x_hbm.at[chunk], x_ref.at[chunk], load_sem.at[chunk])
        for chunk in range(CHUNKS)
    ]
    loads.append(pltpu.make_async_copy(pick_hbm, pick_ref, load_sem.at[CHUNKS]))
    loads.append(pltpu.make_async_copy(bank_hbm, bank_ref, load_sem.at[CHUNKS + 1]))
    for load in loads:
        load.start()
    stores = [
        pltpu.make_async_copy(x_ref.at[chunk], o_hbm.at[chunk], load_sem.at[chunk])
        for chunk in range(CHUNKS)
    ]

    trades = {
        "far in": (FAR, me_far, far_device, far_out, far_in, 0),
        "near in": (NEAR, me_near, near_device, near_out, near_in, 1),
        "near back": (NEAR, me_back, back_device, near_back, near_got, 2),
        "far back": (FAR, me_far, far_device, far_back, far_got, 3),
    }

    def send(name, chunk):
        count, me, device, source, target, kind = trades[name]

        def one(d):
            pltpu.make_async_remote_copy(
                src_ref=source.at[chunk, d],
                dst_ref=target.at[chunk, me],
                send_sem=send_sem.at[kind, chunk],
                recv_sem=recv_sem.at[kind, chunk],
                device_id=device(d),
                device_id_type=MESH,
            ).start()

        around(count, me, one)
        target[chunk, me] = source[chunk, me]

    def whole(name, chunk):
        count, me, device, source, target, kind = trades[name]
        return pltpu.make_async_remote_copy(
            src_ref=source.at[chunk, pl.ds(0, count - 1)],
            dst_ref=target.at[chunk, pl.ds(0, count - 1)],
            send_sem=send_sem.at[kind, chunk],
            recv_sem=recv_sem.at[kind, chunk],
            device_id=device((me + 1) % count),
            device_id_type=MESH,
        )

    def put(name, chunk, value):
        source = trades[name][3]
        source[chunk] = value.reshape(source.shape[1:])

    def got(name, chunk):
        whole(name, chunk).wait_recv()
        return trades[name][4][chunk].reshape(32, 8, 128)

    def matrix(index):
        return turned[0, index], turned[1, index]

    def merged_of(chunk):
        return merged[0, chunk], merged[1, chunk]

    for chunk in range(CHUNKS):
        loads[chunk].wait()
        if chunk in FAR_FIRST:
            put("far in", chunk, first_far(x_ref[chunk]))
        else:
            put("near in", chunk, first_near(x_ref[chunk]))

    pl.semaphore_wait(barrier, FAR + NEAR - 2)
    send("far in", 0)
    send("near in", 2)
    send("far in", 1)
    send("near in", 3)

    loads[CHUNKS].wait()
    loads[CHUNKS + 1].wait()
    for index in range(6):
        pick = (32, 28, 29, 33, 30, 31)[index]
        turned[0, index], turned[1, index] = halves(bank_ref[pick_ref[pick]].T)

    order = halves(lane_order())
    for h in range(CHUNKS):
        merged[0, h], merged[1, h] = halves(product(order, halves(bank_ref[pick_ref[h]])))

    def merge(layer, carry):
        for h in range(CHUNKS):
            total = product(merged_of(h), halves(bank_ref[pick_ref[4 * layer + h]]))
            merged[0, h], merged[1, h] = halves(total)
        return carry

    lax.fori_loop(1, 7, merge, 0)

    def step(come, go, chunk, stage, *more):
        put(go, chunk, stage(got(come, chunk), *more))
        send(go, chunk)

    def finish(come, chunk, stage):
        x_ref[chunk] = stage(got(come, chunk), merged_of(chunk)).reshape(32, 8, 128)
        stores[chunk].start()

    step("near in", "far in", 2, near_then_far)
    step("near in", "far in", 3, near_then_far)
    step("far in", "near in", 0, far_then_near, matrix)
    step("far in", "near in", 1, far_then_near, matrix)
    step("near in", "far back", 0, gates_from_near, matrix)
    step("far in", "near back", 2, gates_from_far, matrix)
    step("near in", "far back", 1, gates_from_near, matrix)
    step("far in", "near back", 3, gates_from_far, matrix)
    step("near back", "far back", 2, back_far)
    step("far back", "near back", 0, back_near)
    step("near back", "far back", 3, back_far)
    step("far back", "near back", 1, back_near)
    finish("near back", 0, last_from_near)
    finish("far back", 2, last_from_far)
    finish("near back", 1, last_from_near)
    finish("far back", 3, last_from_far)
    for name in trades:
        for chunk in range(CHUNKS):
            whole(name, chunk).wait_send()
    for store in stores:
        store.wait()


def per_device(amplitudes, gate_bank, gate_pick):
    far = pltpu.VMEM((CHUNKS, FAR, 8, 128), jnp.float32)
    near = pltpu.VMEM((CHUNKS, NEAR, 4, 8, 128), jnp.float32)
    result = pl.pallas_call(
        kernel,
        out_shape=jax.ShapeDtypeStruct((CHUNKS, 32, 8, 128), jnp.float32),
        in_specs=[
            pl.BlockSpec(memory_space=pltpu.HBM),
            pl.BlockSpec(memory_space=pltpu.HBM),
            pl.BlockSpec(memory_space=pltpu.HBM),
        ],
        out_specs=pl.BlockSpec(memory_space=pltpu.HBM),
        scratch_shapes=[
            pltpu.SMEM(gate_pick.shape, jnp.int32),
            pltpu.VMEM((CHUNKS, 32, 8, 128), jnp.float32),
            pltpu.VMEM(gate_bank.shape, jnp.float32),
            far, far, near, near, near, near, far, far,
            pltpu.VMEM((2, 6, GATE, GATE), jnp.bfloat16),
            pltpu.VMEM((2, CHUNKS, GATE, GATE), jnp.bfloat16),
            pltpu.SemaphoreType.DMA((CHUNKS + 2,)),
            pltpu.SemaphoreType.DMA((4, CHUNKS)),
            pltpu.SemaphoreType.DMA((4, CHUNKS)),
        ],
        compiler_params=pltpu.CompilerParams(
            collective_id=0, has_side_effects=True
        ),
    )(gate_pick, amplitudes.reshape(CHUNKS, 32, 8, 128), gate_bank)
    return result.reshape(amplitudes.shape)


def solution(mesh):
    placed = (P("wide", "narrow", None, None, None, None), P(), P())
    return jax.shard_map(
        per_device,
        mesh=mesh,
        in_specs=placed,
        out_specs=P("wide", "narrow", None, None, None, None),
        check_vma=False,
    )
```

```python
import functools

import jax
import jax.numpy as jnp
from jax import lax
from jax.experimental import pallas as pl
from jax.experimental.pallas import tpu as pltpu
from jax.sharding import PartitionSpec as P

GATE = 128
CHUNKS = 4
FAR = 32
NEAR = 8
FAR_FIRST = (0, 1)
MESH = pl.DeviceIdType.MESH
ROWS_IN = ["r1", "r0", "b2", "b1", "b0"]
LANES_IN = ["a6", "a5", "a4", "a3", "a2", "a1", "a0"]
LANES_OUT = ["a1", "a5", "a4", "a3", "a6", "a2", "a0"]
FAR_ROWS = ["zh", "z2", "z1", "z0", "co"]


def swap(x, row_bit, lane_bit):
    outer, inner, apart = 16 >> row_bit, 8 << row_bit, 1 << lane_bit
    split = x.reshape(outer, 2, inner, 128)
    low, high = split[:, 0].reshape(128, 128), split[:, 1].reshape(128, 128)
    clear = lax.broadcasted_iota(jnp.int32, (128, 128), 1) // apart % 2 == 0
    new_low = jnp.where(clear, low, pltpu.roll(high, apart, 1))
    new_high = jnp.where(clear, pltpu.roll(low, 128 - apart, 1), high)
    parts = [new_low.reshape(outer, 1, inner, 128), new_high.reshape(outer, 1, inner, 128)]
    return jnp.concatenate(parts, axis=1).reshape(32, 8, 128)


class Layout:
    def __init__(self, rows, lanes):
        self.rows, self.lanes = list(rows), list(lanes)

    def exchange(self, x, pairs):
        for row, lane in pairs:
            i, p = self.rows.index(row), self.lanes.index(lane)
            x = swap(x, 4 - i, 6 - p)
            self.rows[i], self.lanes[p] = lane, row
        return x


def halves(x):
    top = x.astype(jnp.bfloat16)
    return top, (x - top.astype(jnp.float32)).astype(jnp.bfloat16)


def product(left, right):
    dot = functools.partial(jnp.dot, preferred_element_type=jnp.float32)
    return dot(left[0], right[0]) + (dot(left[0], right[1]) + dot(left[1], right[0]))


def gate_low(x, matrix):
    wide = jnp.concatenate([x[:16].reshape(128, 128), x[16:].reshape(128, 128)], axis=1)
    y = product(matrix, halves(wide))
    return jnp.concatenate([y[:, :128].reshape(16, 8, 128), y[:, 128:].reshape(16, 8, 128)], axis=0)


def gate_high(x, matrix):
    split = x.reshape(4, 64, 128)
    first = jnp.concatenate([split[0], split[2]], axis=0)
    second = jnp.concatenate([split[1], split[3]], axis=0)
    y = product(matrix, halves(jnp.concatenate([first, second], axis=1)))
    parts = [y[:64, :128], y[:64, 128:], y[64:, :128], y[64:, 128:]]
    return jnp.concatenate([part.reshape(8, 8, 128) for part in parts], axis=0)


def first_far(x):
    at = Layout(ROWS_IN, LANES_IN)
    return at.exchange(x, [("b2", "a6"), ("b1", "a5"), ("b0", "a4")])


def first_near(x):
    at = Layout(ROWS_IN, LANES_IN)
    x = at.exchange(x, [("r1", "a3"), ("r0", "a2"), ("b2", "a1")])
    assert at.rows == ["a3", "a2", "a1", "b1", "b0"]
    return x


def near_then_far(x):
    at = Layout(["x1", "y0", "y1", "b1", "b0"], ["a6", "a5", "a4", "r1", "r0", "b2", "a0"])
    x = at.exchange(x, [("x1", "r1"), ("y0", "r0"), ("y1", "a6"), ("b1", "a5"), ("b0", "a4")])
    assert at.rows == ["r1", "r0", "a6", "a5", "a4"]
    assert at.lanes == ["y1", "b1", "b0", "x1", "y0", "b2", "a0"]
    return x


def far_then_near(x, matrix):
    at = Layout(FAR_ROWS, ["b2", "b1", "b0", "a3", "a2", "a1", "a0"])
    x = gate_low(x, matrix(0))
    return at.exchange(x, [("zh", "a3"), ("z2", "a2"), ("z1", "a1")])


def gates_between(at, x, matrix):
    assert at.rows == ["zh", "y0", "b2", "b1", "b0"]
    assert at.lanes == ["y1", "z0", "co", "x1", "z2", "z1", "a0"]
    x = gate_low(x, matrix(1))
    x = gate_high(x, matrix(2))
    x = at.exchange(x, [("y0", "z2"), ("b2", "z1"), ("b1", "z0"), ("b0", "co")])
    assert at.rows == FAR_ROWS
    x = gate_low(x, matrix(3))
    x = at.exchange(x, [("zh", "x1"), ("z2", "y1"), ("z1", "b2"), ("z0", "b1"), ("co", "b0")])
    assert at.rows == ["x1", "y1", "b2", "b1", "b0"]
    x = gate_low(x, matrix(4))
    return gate_high(x, matrix(5))


def gates_from_near(x, matrix):
    at = Layout(["x1", "y0", "y1", "z0", "co"], ["b2", "b1", "b0", "zh", "z2", "z1", "a0"])
    x = at.exchange(x, [("x1", "zh"), ("y1", "b2"), ("z0", "b1"), ("co", "b0")])
    x = gates_between(at, x, matrix)
    x = at.exchange(x, [("x1", "zh"), ("y1", "z2"), ("b2", "z1"), ("b1", "z0"), ("b0", "co")])
    assert at.rows == FAR_ROWS
    assert at.lanes == ["y1", "b1", "b0", "x1", "y0", "b2", "a0"]
    return x


def gates_from_far(x, matrix):
    at = Layout(FAR_ROWS, ["y1", "b1", "b0", "x1", "y0", "b2", "a0"])
    x = gate_low(x, matrix(0))
    x = at.exchange(x, [("z2", "y0"), ("z1", "b2"), ("z0", "b1"), ("co", "b0")])
    x = gates_between(at, x, matrix)
    x = at.exchange(x, [("b2", "y0")])
    assert at.lanes == ["z2", "z0", "co", "zh", "b2", "z1", "a0"]
    return x


def back_near(x):
    at = Layout(["r1", "r0", "a6", "a5", "a4"], ["y1", "b1", "b0", "x1", "y0", "b2", "a0"])
    x = at.exchange(x, [("r1", "x1"), ("r0", "y1"), ("a6", "y0")])
    assert at.lanes == ["r0", "b1", "b0", "r1", "a6", "b2", "a0"]
    return x


def back_far(x):
    at = Layout(["a3", "a1", "a2", "b1", "b0"], ["z2", "z0", "co", "zh", "b2", "z1", "a0"])
    x = at.exchange(x, [("a3", "zh"), ("a1", "z2"), ("a2", "z1"), ("b1", "z0"), ("b0", "co")])
    assert at.rows == FAR_ROWS
    assert at.lanes == ["a1", "b1", "b0", "a3", "b2", "a2", "a0"]
    return x


def last_from_far(x, merged):
    at = Layout(["r1", "r0", "a6", "a5", "a4"], ["a1", "b1", "b0", "a3", "b2", "a2", "a0"])
    x = at.exchange(x, [("a6", "b2"), ("a5", "b1"), ("a4", "b0")])
    assert at.rows == ROWS_IN and at.lanes == LANES_OUT
    return product(halves(x.reshape(256, 128)), merged)


def last_from_near(x, merged):
    at = Layout(["a3", "a1", "a2", "a5", "a4"], ["r0", "b1", "b0", "r1", "a6", "b2", "a0"])
    x = at.exchange(x, [("a3", "r1"), ("a1", "r0"), ("a2", "b2"), ("a5", "b1"), ("a4", "b0")])
    assert at.rows == ROWS_IN and at.lanes == LANES_OUT
    return product(halves(x.reshape(256, 128)), merged)


def lane_order():
    lane = lax.broadcasted_iota(jnp.int32, (128, 128), 0)
    a = 0
    for place, bit in zip((6, 5, 4, 3, 2, 1, 0), (1, 5, 4, 3, 6, 2, 0)):
        a = a + lane // 2**place % 2 * 2**bit
    return jnp.where(lax.broadcasted_iota(jnp.int32, (128, 128), 1) == a, 1.0, 0.0)


def kernel(
    pick_hbm, x_hbm, bank_hbm, o_ref,
    pick_ref, x_ref, bank_ref,
    far_out, far_in, near_out, near_in, near_back, near_got, far_back, far_got,
    turned, merged, load_sem, send_sem, recv_sem,
):
    w, n = lax.axis_index("wide"), lax.axis_index("narrow")
    me_far = n // 32 * 16 + w
    me_near = n // 16 % 2 * 4 + n % 2 * 2 + n // 2 % 2
    me_back = n // 16 % 2 * 4 + n // 2 % 2 * 2 + n % 2
    rest = n - n // 16 % 2 * 16 - n % 4

    column = n % 32

    def far_device(d):
        upper = jnp.where(d >= 16, 1, 0)
        return {"wide": d - upper * 16, "narrow": column + upper * 32}

    def near_bits(e):
        top = jnp.where(e >= 4, 1, 0)
        low = e - top * 4
        middle = jnp.where(low >= 2, 1, 0)
        return top, middle, low - middle * 2

    def near_device(e):
        top, middle, low = near_bits(e)
        return {"wide": w, "narrow": rest + top * 16 + low * 2 + middle}

    def back_device(e):
        top, middle, low = near_bits(e)
        return {"wide": w, "narrow": rest + top * 16 + middle * 2 + low}

    def around(count, me, each):
        def at(d):
            each(jnp.where(d >= count, d - count, d))

        at(me + count // 2)
        most = count // 2 - 1

        def some(i, carry):
            for step in range(3):
                near = 3 * i + step
                at(me + most - near)
                at(me + count - most + near)
            return carry

        lax.fori_loop(0, most // 3, some, 0)

    barrier = pltpu.get_barrier_semaphore()

    def greet(device):
        pl.semaphore_signal(barrier, inc=1, device_id=device, device_id_type=MESH)

    around(FAR, me_far, lambda d: greet(far_device(d)))
    around(NEAR, me_near, lambda d: greet(near_device(d)))

    loads = [
        pltpu.make_async_copy(x_hbm.at[chunk], x_ref.at[chunk], load_sem.at[chunk])
        for chunk in range(CHUNKS)
    ]
    loads.append(pltpu.make_async_copy(pick_hbm, pick_ref, load_sem.at[CHUNKS]))
    loads.append(pltpu.make_async_copy(bank_hbm, bank_ref, load_sem.at[CHUNKS + 1]))
    for load in loads:
        load.start()
    trades = {
        "far in": (FAR, me_far, far_device, far_out, far_in, 0),
        "near in": (NEAR, me_near, near_device, near_out, near_in, 1),
        "near back": (NEAR, me_back, back_device, near_back, near_got, 2),
        "far back": (FAR, me_far, far_device, far_back, far_got, 3),
    }

    def send(name, chunk):
        count, me, device, source, target, kind = trades[name]

        def one(d):
            pltpu.make_async_remote_copy(
                src_ref=source.at[chunk, d],
                dst_ref=target.at[chunk, me],
                send_sem=send_sem.at[kind, chunk],
                recv_sem=recv_sem.at[kind, chunk],
                device_id=device(d),
                device_id_type=MESH,
            ).start()

        around(count, me, one)
        target[chunk, me] = source[chunk, me]

    def whole(name, chunk):
        count, me, device, source, target, kind = trades[name]
        return pltpu.make_async_remote_copy(
            src_ref=source.at[chunk, pl.ds(0, count - 1)],
            dst_ref=target.at[chunk, pl.ds(0, count - 1)],
            send_sem=send_sem.at[kind, chunk],
            recv_sem=recv_sem.at[kind, chunk],
            device_id=device((me + 1) % count),
            device_id_type=MESH,
        )

    def put(name, chunk, value):
        source = trades[name][3]
        source[chunk] = value.reshape(source.shape[1:])

    def got(name, chunk):
        whole(name, chunk).wait_recv()
        return trades[name][4][chunk].reshape(32, 8, 128)

    def matrix(index):
        return turned[0, index], turned[1, index]

    def merged_of(chunk):
        return merged[0, chunk], merged[1, chunk]

    for chunk in range(CHUNKS):
        loads[chunk].wait()
        if chunk in FAR_FIRST:
            put("far in", chunk, first_far(x_ref[chunk]))
        else:
            put("near in", chunk, first_near(x_ref[chunk]))

    pl.semaphore_wait(barrier, FAR + NEAR - 2)
    send("far in", 0)
    send("near in", 2)
    send("far in", 1)
    send("near in", 3)

    loads[CHUNKS].wait()
    loads[CHUNKS + 1].wait()
    for index in range(6):
        pick = (32, 28, 29, 33, 30, 31)[index]
        turned[0, index], turned[1, index] = halves(bank_ref[pick_ref[pick]].T)

    order = halves(lane_order())
    for h in range(CHUNKS):
        merged[0, h], merged[1, h] = halves(product(order, halves(bank_ref[pick_ref[h]])))

    def merge(layer, carry):
        for h in range(CHUNKS):
            total = product(merged_of(h), halves(bank_ref[pick_ref[4 * layer + h]]))
            merged[0, h], merged[1, h] = halves(total)
        return carry

    lax.fori_loop(1, 7, merge, 0)

    def step(come, go, chunk, stage, *more):
        put(go, chunk, stage(got(come, chunk), *more))
        send(go, chunk)

    def finish(come, chunk, stage):
        o_ref[chunk] = stage(got(come, chunk), merged_of(chunk)).reshape(32, 8, 128)

    step("near in", "far in", 2, near_then_far)
    step("near in", "far in", 3, near_then_far)
    step("far in", "near in", 0, far_then_near, matrix)
    step("far in", "near in", 1, far_then_near, matrix)
    step("near in", "far back", 0, gates_from_near, matrix)
    step("far in", "near back", 2, gates_from_far, matrix)
    step("near in", "far back", 1, gates_from_near, matrix)
    step("far in", "near back", 3, gates_from_far, matrix)
    step("near back", "far back", 2, back_far)
    step("far back", "near back", 0, back_near)
    step("near back", "far back", 3, back_far)
    step("far back", "near back", 1, back_near)
    finish("near back", 0, last_from_near)
    finish("far back", 2, last_from_far)
    finish("near back", 1, last_from_near)
    finish("far back", 3, last_from_far)
    for name in trades:
        for chunk in range(CHUNKS):
            whole(name, chunk).wait_send()


def per_device(amplitudes, gate_bank, gate_pick):
    far = pltpu.VMEM((CHUNKS, FAR, 8, 128), jnp.float32)
    near = pltpu.VMEM((CHUNKS, NEAR, 4, 8, 128), jnp.float32)
    result = pl.pallas_call(
        kernel,
        out_shape=jax.ShapeDtypeStruct((CHUNKS, 32, 8, 128), jnp.float32),
        in_specs=[
            pl.BlockSpec(memory_space=pltpu.HBM),
            pl.BlockSpec(memory_space=pltpu.HBM),
            pl.BlockSpec(memory_space=pltpu.HBM),
        ],
        out_specs=pl.BlockSpec(memory_space=pltpu.VMEM),
        scratch_shapes=[
            pltpu.SMEM(gate_pick.shape, jnp.int32),
            pltpu.VMEM((CHUNKS, 32, 8, 128), jnp.float32),
            pltpu.VMEM(gate_bank.shape, jnp.float32),
            far, far, near, near, near, near, far, far,
            pltpu.VMEM((2, 6, GATE, GATE), jnp.bfloat16),
            pltpu.VMEM((2, CHUNKS, GATE, GATE), jnp.bfloat16),
            pltpu.SemaphoreType.DMA((CHUNKS + 2,)),
            pltpu.SemaphoreType.DMA((4, CHUNKS)),
            pltpu.SemaphoreType.DMA((4, CHUNKS)),
        ],
        compiler_params=pltpu.CompilerParams(
            collective_id=0, has_side_effects=True, vmem_limit_bytes=32 << 20
        ),
    )(
        *(
            pltpu.with_memory_space_constraint(operand, pltpu.HBM)
            for operand in (gate_pick, amplitudes.reshape(CHUNKS, 32, 8, 128), gate_bank)
        )
    )
    return result.reshape(amplitudes.shape)


def solution(mesh):
    placed = (P("wide", "narrow", None, None, None, None), P(), P())
    return jax.shard_map(
        per_device,
        mesh=mesh,
        in_specs=placed,
        out_specs=P("wide", "narrow", None, None, None, None),
        check_vma=False,
    )
```

```python
import functools

import jax
import jax.numpy as jnp
from jax import lax
from jax.experimental import pallas as pl
from jax.experimental.pallas import tpu as pltpu
from jax.sharding import PartitionSpec as P

GATE = 128
CHUNKS = 4
FAR = 32
NEAR = 8
MIXED = 16
FAR_FIRST = (0, 1)
MESH = pl.DeviceIdType.MESH
ROWS_IN = ["r1", "r0", "b2", "b1", "b0"]
LANES_IN = ["a6", "a5", "a4", "a3", "a2", "a1", "a0"]
LANES_OUT = ["a1", "a5", "a4", "a3", "a6", "a2", "a0"]
FAR_ROWS = ["zh", "z2", "z1", "z0", "co"]


def swap(x, row_bit, lane_bit):
    outer, inner, apart = 16 >> row_bit, 8 << row_bit, 1 << lane_bit
    split = x.reshape(outer, 2, inner, 128)
    low, high = split[:, 0].reshape(128, 128), split[:, 1].reshape(128, 128)
    clear = lax.broadcasted_iota(jnp.int32, (128, 128), 1) // apart % 2 == 0
    new_low = jnp.where(clear, low, pltpu.roll(high, apart, 1))
    new_high = jnp.where(clear, pltpu.roll(low, 128 - apart, 1), high)
    parts = [new_low.reshape(outer, 1, inner, 128), new_high.reshape(outer, 1, inner, 128)]
    return jnp.concatenate(parts, axis=1).reshape(32, 8, 128)


class Layout:
    def __init__(self, rows, lanes):
        self.rows, self.lanes = list(rows), list(lanes)

    def exchange(self, x, pairs):
        for row, lane in pairs:
            i, p = self.rows.index(row), self.lanes.index(lane)
            x = swap(x, 4 - i, 6 - p)
            self.rows[i], self.lanes[p] = lane, row
        return x


def halves(x):
    top = x.astype(jnp.bfloat16)
    return top, (x - top.astype(jnp.float32)).astype(jnp.bfloat16)


def product(left, right):
    dot = functools.partial(jnp.dot, preferred_element_type=jnp.float32)
    return dot(left[0], right[0]) + (dot(left[0], right[1]) + dot(left[1], right[0]))


def gate_low(x, matrix):
    wide = jnp.concatenate([x[:16].reshape(128, 128), x[16:].reshape(128, 128)], axis=1)
    y = product(matrix, halves(wide))
    return jnp.concatenate([y[:, :128].reshape(16, 8, 128), y[:, 128:].reshape(16, 8, 128)], axis=0)


def gate_high(x, matrix):
    split = x.reshape(4, 64, 128)
    first = jnp.concatenate([split[0], split[2]], axis=0)
    second = jnp.concatenate([split[1], split[3]], axis=0)
    y = product(matrix, halves(jnp.concatenate([first, second], axis=1)))
    parts = [y[:64, :128], y[:64, 128:], y[64:, :128], y[64:, 128:]]
    return jnp.concatenate([part.reshape(8, 8, 128) for part in parts], axis=0)


def first_far(x):
    at = Layout(ROWS_IN, LANES_IN)
    return at.exchange(x, [("b2", "a6"), ("b1", "a5"), ("b0", "a4")])


def first_near(x):
    at = Layout(ROWS_IN, LANES_IN)
    x = at.exchange(x, [("r1", "a3"), ("r0", "a2"), ("b2", "a1"), ("b1", "a4")])
    assert at.rows == ["a3", "a2", "a1", "a4", "b0"]
    return x


def near_then_far(x):
    at = Layout(["x1", "y0", "y1", "co", "b0"], ["a6", "a5", "b1", "r1", "r0", "b2", "a0"])
    x = at.exchange(x, [("x1", "r1"), ("y0", "r0"), ("y1", "a6"), ("co", "a5")])
    assert at.rows == ["r1", "r0", "a6", "a5", "b0"]
    return x


def far_then_near(x, matrix):
    at = Layout(FAR_ROWS, ["b2", "b1", "b0", "a3", "a2", "a1", "a0"])
    x = gate_low(x, matrix(0))
    return at.exchange(x, [("zh", "a3"), ("z2", "a2"), ("z1", "a1")])


def gates_between(at, x, matrix):
    assert at.rows == ["zh", "y0", "b2", "b1", "b0"]
    x = gate_low(x, matrix(1))
    x = gate_high(x, matrix(2))
    x = at.exchange(x, [("y0", "z2"), ("b2", "z1"), ("b1", "z0"), ("b0", "co")])
    assert at.rows == FAR_ROWS
    x = gate_low(x, matrix(3))
    x = at.exchange(x, [("zh", "x1"), ("z2", "y1"), ("z1", "b2"), ("z0", "b1"), ("co", "b0")])
    assert at.rows == ["x1", "y1", "b2", "b1", "b0"]
    x = gate_low(x, matrix(4))
    return gate_high(x, matrix(5))


def gates_from_near(x, matrix):
    at = Layout(["x1", "y0", "y1", "z0", "co"], ["b2", "b1", "b0", "zh", "z2", "z1", "a0"])
    x = at.exchange(x, [("x1", "zh"), ("y1", "b2"), ("z0", "b1"), ("co", "b0")])
    x = gates_between(at, x, matrix)
    x = at.exchange(x, [("x1", "zh"), ("y1", "z2"), ("b2", "z1"), ("b1", "z0"), ("b0", "co")])
    assert at.rows == FAR_ROWS
    assert at.lanes == ["y1", "b1", "b0", "x1", "y0", "b2", "a0"]
    return x


def gates_from_far(x, matrix):
    at = Layout(["zh", "z2", "z1", "z0", "b0"], ["y1", "co", "b1", "x1", "y0", "b2", "a0"])
    x = at.exchange(x, [("b0", "co")])
    x = gate_low(x, matrix(0))
    x = at.exchange(x, [("z2", "y0"), ("z1", "b2"), ("z0", "b1"), ("co", "b0")])
    x = gates_between(at, x, matrix)
    x = at.exchange(x, [("b2", "y0"), ("b1", "co")])
    assert at.rows == ["x1", "y1", "y0", "co", "b0"]
    assert at.lanes == ["z2", "b1", "z0", "zh", "b2", "z1", "a0"]
    return x


def back_near(x):
    at = Layout(["r1", "r0", "a6", "a5", "a4"], ["y1", "b1", "b0", "x1", "y0", "b2", "a0"])
    x = at.exchange(x, [("r1", "x1"), ("r0", "y1"), ("a6", "y0")])
    assert at.lanes == ["r0", "b1", "b0", "r1", "a6", "b2", "a0"]
    return x


def back_far(x):
    at = Layout(["a3", "a1", "a2", "a4", "b0"], ["z2", "b1", "z0", "zh", "b2", "z1", "a0"])
    x = at.exchange(x, [("a3", "zh"), ("a1", "z2"), ("a2", "z1"), ("a4", "z0")])
    assert at.lanes == ["a1", "b1", "a4", "a3", "b2", "a2", "a0"]
    return x


def last_from_far(x, merged):
    at = Layout(["r1", "r0", "a6", "a5", "b0"], ["a1", "b1", "a4", "a3", "b2", "a2", "a0"])
    x = at.exchange(x, [("a6", "b2"), ("a5", "b1")])
    assert at.rows == ROWS_IN and at.lanes == LANES_OUT
    return product(halves(x.reshape(256, 128)), merged)


def last_from_near(x, merged):
    at = Layout(["a3", "a1", "a2", "a5", "a4"], ["r0", "b1", "b0", "r1", "a6", "b2", "a0"])
    x = at.exchange(x, [("a3", "r1"), ("a1", "r0"), ("a2", "b2"), ("a5", "b1"), ("a4", "b0")])
    assert at.rows == ROWS_IN and at.lanes == LANES_OUT
    return product(halves(x.reshape(256, 128)), merged)


def lane_order():
    lane = lax.broadcasted_iota(jnp.int32, (128, 128), 0)
    a = 0
    for place, bit in zip((6, 5, 4, 3, 2, 1, 0), (1, 5, 4, 3, 6, 2, 0)):
        a = a + lane // 2**place % 2 * 2**bit
    return jnp.where(lax.broadcasted_iota(jnp.int32, (128, 128), 1) == a, 1.0, 0.0)


def kernel(
    pick_hbm, x_hbm, bank_hbm, o_ref,
    pick_ref, x_ref, bank_ref,
    far_out, far_in, near_out, near_in, near_back, near_got, far_back, far_got,
    m0, m1, m2, m3, m4, m5, m6, m7,
    turned, merged, load_sem, send_sem, recv_sem,
):
    mixed = (m0, m1, m2, m3, m4, m5, m6, m7)
    w, n = lax.axis_index("wide"), lax.axis_index("narrow")
    me_far = n // 32 * 16 + w
    me_near = n // 16 % 2 * 4 + n % 2 * 2 + n // 2 % 2
    me_back = n // 16 % 2 * 4 + n // 2 % 2 * 2 + n % 2
    rest = n - n // 16 % 2 * 16 - n % 4

    column = n % 32

    def far_device(d):
        upper = jnp.where(d >= 16, 1, 0)
        return {"wide": d - upper * 16, "narrow": column + upper * 32}

    def near_bits(e):
        top = jnp.where(e >= 4, 1, 0)
        low = e - top * 4
        middle = jnp.where(low >= 2, 1, 0)
        return top, middle, low - middle * 2

    def near_device(e):
        top, middle, low = near_bits(e)
        return {"wide": w, "narrow": rest + top * 16 + low * 2 + middle}

    def back_device(e):
        top, middle, low = near_bits(e)
        return {"wide": w, "narrow": rest + top * 16 + middle * 2 + low}

    core = w % 2
    me_ring = n // 32 * 8 + w // 2
    me_side, me_side_back = me_near * 2 + core, me_back * 2 + core

    def ring_device(d):
        upper = jnp.where(d >= 8, 1, 0)
        return {"wide": d * 2 - upper * 16 + core, "narrow": column + upper * 32}

    def side_bits(e):
        top = jnp.where(e >= 8, 1, 0)
        e = e - top * 8
        second = jnp.where(e >= 4, 1, 0)
        e = e - second * 4
        third = jnp.where(e >= 2, 1, 0)
        return top, second, third, w - core + e - third * 2

    def side_device(e):
        top, second, third, place = side_bits(e)
        return {"wide": place, "narrow": rest + top * 16 + third * 2 + second}

    def side_back_device(e):
        top, second, third, place = side_bits(e)
        return {"wide": place, "narrow": rest + top * 16 + second * 2 + third}

    def around(count, me, each):
        def at(d):
            each(jnp.where(d >= count, d - count, d))

        at(me + count // 2)
        most = count // 2 - 1

        steps = 3 if most % 3 == 0 else 1

        def some(i, carry):
            for step in range(steps):
                near = steps * i + step
                at(me + most - near)
                at(me + count - most + near)
            return carry

        lax.fori_loop(0, most // steps, some, 0)

    barrier = pltpu.get_barrier_semaphore()

    def greet(device):
        pl.semaphore_signal(barrier, inc=1, device_id=device, device_id_type=MESH)

    around(FAR, me_far, lambda d: greet(far_device(d)))
    around(MIXED, me_side, lambda d: greet(side_device(d)))

    loads = [
        pltpu.make_async_copy(x_hbm.at[chunk], x_ref.at[chunk], load_sem.at[chunk])
        for chunk in range(CHUNKS)
    ]
    loads.append(pltpu.make_async_copy(pick_hbm, pick_ref, load_sem.at[CHUNKS]))
    loads.append(pltpu.make_async_copy(bank_hbm, bank_ref, load_sem.at[CHUNKS + 1]))
    for load in loads:
        load.start()
    first = {
        "far in": (FAR, me_far, far_device, far_out, far_in, 0),
        "near in": (NEAR, me_near, near_device, near_out, near_in, 1),
        "near back": (NEAR, me_back, back_device, near_back, near_got, 2),
        "far back": (FAR, me_far, far_device, far_back, far_got, 3),
    }
    second = {
        "far in": (MIXED, me_ring, ring_device, mixed[0], mixed[1], 0),
        "near in": (MIXED, me_side, side_device, mixed[2], mixed[3], 1),
        "near back": (MIXED, me_side_back, side_back_device, mixed[4], mixed[5], 2),
        "far back": (MIXED, me_ring, ring_device, mixed[6], mixed[7], 3),
    }

    def trade(name, chunk):
        count, me, device, source, target, kind = (first if chunk in FAR_FIRST else second)[name]
        return count, me, device, source.at[chunk % 2], target.at[chunk % 2], kind

    def send(name, chunk):
        count, me, device, source, target, kind = trade(name, chunk)

        def one(d):
            pltpu.make_async_remote_copy(
                src_ref=source.at[d],
                dst_ref=target.at[me],
                send_sem=send_sem.at[kind, chunk],
                recv_sem=recv_sem.at[kind, chunk],
                device_id=device(d),
                device_id_type=MESH,
            ).start()

        around(count, me, one)
        target[me] = source[me]

    def whole(name, chunk):
        count, me, device, source, target, kind = trade(name, chunk)
        return pltpu.make_async_remote_copy(
            src_ref=source.at[pl.ds(0, count - 1)],
            dst_ref=target.at[pl.ds(0, count - 1)],
            send_sem=send_sem.at[kind, chunk],
            recv_sem=recv_sem.at[kind, chunk],
            device_id=device((me + 1) % count),
            device_id_type=MESH,
        )

    def put(name, chunk, value):
        source = trade(name, chunk)[3]
        source[...] = value.reshape(source.shape)

    def got(name, chunk):
        whole(name, chunk).wait_recv()
        return trade(name, chunk)[4][...].reshape(32, 8, 128)

    def matrix(index):
        return turned[0, index], turned[1, index]

    def merged_of(chunk):
        return merged[0, chunk], merged[1, chunk]

    for chunk in range(CHUNKS):
        loads[chunk].wait()
        if chunk in FAR_FIRST:
            put("far in", chunk, first_far(x_ref[chunk]))
        else:
            put("near in", chunk, first_near(x_ref[chunk]))

    pl.semaphore_wait(barrier, FAR + MIXED - 2)
    send("far in", 0)
    send("near in", 2)
    send("far in", 1)
    send("near in", 3)

    loads[CHUNKS].wait()
    loads[CHUNKS + 1].wait()
    for index in range(6):
        pick = (32, 28, 29, 33, 30, 31)[index]
        turned[0, index], turned[1, index] = halves(bank_ref[pick_ref[pick]].T)

    order = halves(lane_order())
    for h in range(CHUNKS):
        merged[0, h], merged[1, h] = halves(product(order, halves(bank_ref[pick_ref[h]])))

    def merge(layer, carry):
        for h in range(CHUNKS):
            total = product(merged_of(h), halves(bank_ref[pick_ref[4 * layer + h]]))
            merged[0, h], merged[1, h] = halves(total)
        return carry

    lax.fori_loop(1, 7, merge, 0)

    def step(come, go, chunk, stage, *more):
        put(go, chunk, stage(got(come, chunk), *more))
        send(go, chunk)

    def finish(come, chunk, stage):
        o_ref[chunk] = stage(got(come, chunk), merged_of(chunk)).reshape(32, 8, 128)

    step("near in", "far in", 2, near_then_far)
    step("near in", "far in", 3, near_then_far)
    step("far in", "near in", 0, far_then_near, matrix)
    step("far in", "near in", 1, far_then_near, matrix)
    step("near in", "far back", 0, gates_from_near, matrix)
    step("far in", "near back", 2, gates_from_far, matrix)
    step("near in", "far back", 1, gates_from_near, matrix)
    step("far in", "near back", 3, gates_from_far, matrix)
    step("near back", "far back", 2, back_far)
    step("far back", "near back", 0, back_near)
    step("near back", "far back", 3, back_far)
    step("far back", "near back", 1, back_near)
    finish("near back", 0, last_from_near)
    finish("far back", 2, last_from_far)
    finish("near back", 1, last_from_near)
    finish("far back", 3, last_from_far)
    for name in first:
        for chunk in range(CHUNKS):
            whole(name, chunk).wait_send()


def per_device(amplitudes, gate_bank, gate_pick):
    far = pltpu.VMEM((2, FAR, 8, 128), jnp.float32)
    near = pltpu.VMEM((2, NEAR, 4, 8, 128), jnp.float32)
    mixed = pltpu.VMEM((2, MIXED, 2, 8, 128), jnp.float32)
    result = pl.pallas_call(
        kernel,
        out_shape=jax.ShapeDtypeStruct((CHUNKS, 32, 8, 128), jnp.float32),
        in_specs=[
            pl.BlockSpec(memory_space=pltpu.HBM),
            pl.BlockSpec(memory_space=pltpu.HBM),
            pl.BlockSpec(memory_space=pltpu.HBM),
        ],
        out_specs=pl.BlockSpec(memory_space=pltpu.VMEM),
        scratch_shapes=[
            pltpu.SMEM(gate_pick.shape, jnp.int32),
            pltpu.VMEM((CHUNKS, 32, 8, 128), jnp.float32),
            pltpu.VMEM(gate_bank.shape, jnp.float32),
            far, far, near, near, near, near, far, far,
            *[mixed] * 8,
            pltpu.VMEM((2, 6, GATE, GATE), jnp.bfloat16),
            pltpu.VMEM((2, CHUNKS, GATE, GATE), jnp.bfloat16),
            pltpu.SemaphoreType.DMA((CHUNKS + 2,)),
            pltpu.SemaphoreType.DMA((4, CHUNKS)),
            pltpu.SemaphoreType.DMA((4, CHUNKS)),
        ],
        compiler_params=pltpu.CompilerParams(
            collective_id=0, has_side_effects=True, vmem_limit_bytes=32 << 20
        ),
    )(
        *(
            pltpu.with_memory_space_constraint(operand, pltpu.HBM)
            for operand in (gate_pick, amplitudes.reshape(CHUNKS, 32, 8, 128), gate_bank)
        )
    )
    return result.reshape(amplitudes.shape)


def solution(mesh):
    placed = (P("wide", "narrow", None, None, None, None), P(), P())
    return jax.shard_map(
        per_device,
        mesh=mesh,
        in_specs=placed,
        out_specs=P("wide", "narrow", None, None, None, None),
        check_vma=False,
    )
```
